512 devices in a mesh: occ: 16 (over x, z_hi), aux: 32 (over z_lo, y, core).
Axes of the slice: x: 4, y: 4, z: 16 (z_hi: 4, z_lo: 4; z = z_hi * 4 + z_lo), core: 2. Of those that a mesh axis runs over, the one named last changes fastest.
Arguments:
- integrals: bfloat16 [16384, 64, 256], P(('aux', 'occ')), may hold values from -0.59765625 to 0.59765625
- eps_occ: float32 [1024], replicated, may hold values from -3 to -0.5
- eps_vir: float32 [4096], replicated, may hold values from 0.5 to 4
- src_occ: int32 [4], replicated, may hold values from 0 to 63
- occ_offset: int32 [1], replicated, may hold values from 0 to 960
- vir_offset: int32 [1], replicated, may hold values from 0 to 3840
Outputs:
- density: bfloat16 [16384, 64, 256], P('aux', 'occ')
The draws below stay inside these ranges and needn't reach their ends.
Inputs may be any that keep to these rules, and one draw needn't show every extreme that they name: `src_occ`: each entry is an occupied index inside the window. `occ_offset`: the window of 64 occupied orbitals lies inside the occupied energies. `vir_offset`: the block of 256 virtual orbitals lies inside the virtual energies.
All inputs are finite; a program needn't handle non-finite values.
Results may differ from the reference program's by a relative error of at most 0.009.
Values may be sent and summed in bfloat16 or wider, within the bound.
A program may use at most 64 MiB of HBM per device.

```python
import jax
import jax.numpy as jnp
from jax import lax

NAUX = 16384
NOCC = 1024
NVIRT = 4096
NVB = 256
NSRC = 4
NOW = 64
N_AUX = 32


def touch_ends(entries, stream_key, least, largest):
    longest = entries.shape.index(max(entries.shape))
    spots = []
    for shift in (0, 1):
        where = [jax.random.randint(jax.random.fold_in(stream_key, axis), (), 0, length) for axis, length in enumerate(entries.shape)]
        where[longest] = (where[longest] + shift) % entries.shape[longest]
        spots.append(tuple(where))
    return entries.at[spots[0]].set(least).at[spots[1]].set(largest)


def block_scale(rng, dims, shards, least, largest):
    loudness = 1.0
    for dim, parts in shards:
        steps = jax.random.uniform(jax.random.fold_in(jax.random.fold_in(rng, 6), dim), (parts,), jnp.float32, least / len(shards), largest / len(shards))
        loudness = loudness * jnp.repeat(jnp.exp(steps), dims[dim] // parts).reshape((-1,) + (1,) * (len(dims) - 1 - dim))
    return loudness


def centred(rng, dims, width, most, shards=(), dtype=jnp.bfloat16):
    loudness = block_scale(rng, dims, shards, -0.22, 0.18) if shards else 1.0
    values = jax.random.normal(rng, dims, jnp.float32) * width * loudness
    return jnp.minimum(jnp.maximum(values, -most), most).astype(dtype)


def setup_inputs(seed: int = 0) -> dict:
    key_of = jax.random.split(jax.random.key(seed), 7)
    integrals = centred(key_of[0], (NAUX, NOW, NVB), 0.09, 0.59765625, ((0, 512),))
    eps_occ = jnp.clip(jax.random.uniform(key_of[1], (NOCC,), jnp.float32, -3.0, -0.5), -3.0, -0.5)
    eps_vir = jnp.clip(jax.random.uniform(key_of[2], (NVIRT,), jnp.float32, 0.5, 4.0), 0.5, 4.0)
    src_occ = touch_ends(jax.random.randint(key_of[3], (NSRC,), 0, NOW), jax.random.fold_in(key_of[3], 1), 0, NOW - 1).astype(jnp.int32)
    occ_offset = jax.random.randint(key_of[4], (1,), 0, NOCC - NOW + 1).astype(jnp.int32)
    vir_offset = jax.random.randint(key_of[5], (1,), 0, NVIRT - NVB + 1).astype(jnp.int32)
    return {"integrals": integrals, "eps_occ": eps_occ, "eps_vir": eps_vir, "src_occ": src_occ, "occ_offset": occ_offset, "vir_offset": vir_offset}


def reference(integrals, eps_occ, eps_vir, src_occ, occ_offset, vir_offset):
    aux_total, occ_count, virt_count = integrals.shape
    group_rows = aux_total // N_AUX
    grouped = integrals.reshape(N_AUX, group_rows, occ_count * virt_count)
    occ_energy = lax.dynamic_slice_in_dim(eps_occ, occ_offset[0], occ_count)
    vir_energy = lax.dynamic_slice_in_dim(eps_vir, vir_offset[0], virt_count)
    amplitudes = []
    sources = []
    for source_step in range(NSRC):
        src_index = src_occ[source_step]
        source = lax.dynamic_index_in_dim(integrals, src_index, 1, keepdims=False)
        source_groups = source.reshape(N_AUX, group_rows, virt_count)

        def add_group(carry, pair_in):
            block_ints, block_src = pair_in
            term = lax.dot_general(block_ints, block_src, (((0,), (0,)), ((), ())), preferred_element_type=jnp.float32)
            return carry + term, None

        start = jnp.zeros((occ_count * virt_count, virt_count), jnp.float32)
        pair_sum, _ = lax.scan(add_group, start, (grouped, source_groups))
        pair_sum = pair_sum.reshape(occ_count, virt_count, virt_count)
        src_energy = lax.dynamic_index_in_dim(eps_occ, occ_offset[0] + src_index, 0, keepdims=False)
        denom = vir_energy[None, :, None] + vir_energy[None, None, :] - occ_energy[:, None, None] - src_energy
        scaled = (pair_sum / denom).astype(jnp.bfloat16).astype(jnp.float32)
        amplitude = (2.0 * scaled - jnp.transpose(scaled, (0, 2, 1))).astype(jnp.bfloat16)
        amplitudes.append(amplitude.reshape(occ_count * virt_count, virt_count))
        sources.append(source_groups)
    amp_stack = jnp.stack(amplitudes)
    src_stack = jnp.stack(sources, axis=1)

    def density_group(src_group):
        total = jnp.zeros((group_rows, occ_count * virt_count), jnp.float32)
        for source_step in range(NSRC):
            total = total + lax.dot_general(src_group[source_step], amp_stack[source_step], (((1,), (1,)), ((), ())), preferred_element_type=jnp.float32)
        return total.astype(jnp.bfloat16)

    result = lax.map(density_group, src_stack)
    return result.reshape(aux_total, occ_count, virt_count)
```

```python
import jax
import jax.numpy as jnp
from jax import lax
from jax.experimental import pallas as pl
from jax.experimental.pallas import tpu as pltpu
from jax.sharding import PartitionSpec as P

MESH = pl.DeviceIdType.MESH
F32, BF16 = jnp.float32, jnp.bfloat16


def coords():
    occ, aux = lax.axis_index("occ"), lax.axis_index("aux")
    return occ // 4, (aux // 2) % 4, (occ % 4) * 4 + aux // 8, aux % 2


def device(x, y, z, c):
    return {"occ": x * 4 + z // 4, "aux": ((z % 4) * 4 + y) * 2 + c}


A0, SRC1, SRC2, FWD, ZG, XG, RING, XCH, AZ, AY, AC, LOCAL, COUNT = (
    0, 32, 38, 44, 52, 55, 58, 90, 91, 94, 106, 122, 125,
)
ORDER = (1, 3, 2)


def kernel(a_ref, s_ref, den_ref, d_ref, ar, at, sr, sd, cc, rb, sb, s16, xb, amp, dacc, snd, rcv):
    x, y, z, c = coords()
    zh, zl = z // 4, z % 4

    def copy(src, dst, slot, dev):
        return pltpu.make_async_remote_copy(
            src_ref=src, dst_ref=dst, send_sem=snd.at[slot], recv_sem=rcv.at[slot],
            device_id=dev, device_id_type=MESH,
        )

    barrier = pltpu.get_barrier_semaphore()

    def greet(dev):
        pl.semaphore_signal(barrier, inc=1, device_id=dev, device_id_type=MESH)

    def plane(o):
        return device((x + o // 8) % 4, (y + (o // 2) % 4) % 4, z, (c + o) % 2)

    @pl.loop(1, 32)
    def _(o):
        greet(plane(o))

    greet(device(x, y, (z + 1) % 16, c))
    greet(device(x, y, (z + 15) % 16, c))
    for j in (1, 2, 3):
        greet(device(x, y, (z + 4 * j) % 16, c))
        greet(device(x, y, zh * 4 + (zl + j) % 4, c))
    pl.semaphore_wait(barrier, 39)

    locals_ = [
        pltpu.make_async_copy(a_ref.at[x, :, y, c], ar.at[:, x, y, c], rcv.at[LOCAL]),
        pltpu.make_async_copy(s_ref, sr.at[:, x, y, c], rcv.at[LOCAL + 1]),
        pltpu.make_async_copy(s_ref, sd.at[:, x, zh], rcv.at[LOCAL + 2]),
    ]
    for cp in locals_:
        cp.start()

    xs = {j: (x + j) % 4 for j in (1, 2, 3)}
    ys = {j: (y + j) % 4 for j in (1, 2, 3)}
    first = [
        (copy(s_ref.at[0:2], sr.at[0:2, x, y, c], SRC1 + j - 1, device(xs[j], y, z, c)),
         copy(s_ref.at[2:4], sr.at[2:4, x, y, c], SRC1 + 2 + j, device(x, ys[j], z, c)))
        for j in ORDER
    ]
    for p, q in first:
        p.start()
        q.start()
    zg = [copy(s_ref, sd.at[:, x, zh], ZG + j - 1, device(x, y, (z + 4 * j) % 16, c)) for j in ORDER]
    for cp in zg:
        cp.start()

    def a_copy(o):
        tx, ty, tc = (x + o // 8) % 4, (y + (o // 2) % 4) % 4, (c + o) % 2
        return copy(a_ref.at[tx, :, ty, tc], ar.at[:, x, y, c], A0 + o, device(tx, ty, z, tc))

    @pl.loop(1, 32)
    def _(o):
        a_copy(o).start()

    for cp in locals_:
        cp.wait()
    other = device(x, y, z, 1 - c)
    fwd = []

    def forward(view, slot):
        cp = copy(view, view, slot, other)
        cp.start()
        fwd.append(cp)

    for p, q in first:
        p.wait_recv()
        q.wait_recv()
    vx, vy = sr.at[0:2, :, y, c], sr.at[2:4, x, :, c]
    second = []
    for j in ORDER:
        p = copy(vx, vx, SRC2 + j - 1, device(x, ys[j], z, c))
        q = copy(vy, vy, SRC2 + 2 + j, device(xs[j], y, z, c))
        p.start()
        q.start()
        second.append((p, q))
    forward(vx, FWD)
    forward(vy, FWD + 1)
    for n, j in enumerate(ORDER):
        p, q = second[n]
        p.wait_recv()
        forward(sr.at[0:2, :, (y + 4 - j) % 4, c], FWD + 2 + 2 * n)
        q.wait_recv()
        forward(sr.at[2:4, (x + 4 - j) % 4, :, c], FWD + 3 + 2 * n)

    @pl.loop(1, 32)
    def _(o):
        a_copy(o).wait_recv()

    @pl.loop(0, 4)
    def _(h):
        at[pl.ds(h * 128, 128), :] = ar[h].reshape(1024, 128).T

    for cp in zg:
        cp.wait_recv()
    vd = sd.at[:, x]
    xg = [copy(vd, vd, XG + j - 1, device(xs[j], y, z, c)) for j in ORDER]
    for cp in xg:
        cp.start()

    for cp in fwd:
        cp.wait_recv()

    @pl.loop(0, 4)
    def _(s):
        part = jnp.dot(at[...], sr[s].reshape(1024, 256), preferred_element_type=F32)
        for h in range(4):
            cc[h * 4 + s] = part[h * 128:(h + 1) * 128]

    up, down = device(x, y, (z + 1) % 16, c), device(x, y, (z + 15) % 16, c)

    def hop(way, d, q):
        return copy(sb.at[way, d - 1, q], rb.at[way, d - 1, q], RING + (way * 8 + d - 1) * 2 + q, up if way == 0 else down)

    def arrived(way, d, q):
        hop(way, d + 1, q).wait_recv()

    def send(way, d, q, add):
        target = (z + d) % 16 if way == 0 else (z + 16 - d) % 16
        value = cc[target, pl.ds(q * 64, 64), :]
        if add:
            arrived(way, d, q)
            value = value + rb[way, d, q].astype(F32)
        sb[way, d - 1, q] = value.astype(BF16)
        hop(way, d, q).start()

    for q in (0, 1):
        send(0, 8, q, False)
        send(1, 7, q, False)

    @pl.loop(1, 7)
    def _(k):
        for q in (0, 1):
            send(0, 8 - k, q, True)
            send(1, 7 - k, q, True)

    for q in (0, 1):
        send(0, 1, q, True)

    for q in (0, 1):
        rows = pl.ds(q * 64, 64)
        arrived(1, 0, q)
        total = cc[z, rows, :] + rb[1, 0, q].astype(F32)
        arrived(0, 0, q)
        total = total + rb[0, 0, q].astype(F32)
        s16[rows, :] = (total / den_ref[rows, :]).astype(BF16)

    mine, theirs = pl.ds(pl.multiple_of(c * 128, 128), 128), pl.ds(pl.multiple_of((1 - c) * 128, 128), 128)
    xch = copy(s16.at[:, theirs], xb, XCH, other)
    xch.start()
    own = amp.at[y * 4 + zl, c]
    s_mine = s16[:, mine].astype(F32)
    own[:, mine] = (2.0 * s_mine - s_mine.T).astype(BF16)
    xch.wait_recv()
    own[:, theirs] = (2.0 * s16[:, theirs].astype(F32) - xb[...].astype(F32).T).astype(BF16)

    def to_z(j):
        return copy(own, own, AZ + j - 1, device(x, y, zh * 4 + (zl + j) % 4, c))

    def block(j, m):
        return (y + 4 - m) % 4 * 4 + (zl + 4 - j) % 4

    def to_y(j, m):
        view = amp.at[block(j, 0), c]
        return copy(view, view, AY + j * 3 + m - 1, device(x, (y + m) % 4, z, c))

    def to_core(j, m):
        view = amp.at[block(j, m), c]
        return copy(view, view, AC + j * 4 + m, other)

    for j in ORDER:
        to_z(j).start()
    for j in (0, 1, 3, 2):
        if j:
            to_z(j).wait_recv()
        for m in ORDER:
            to_y(j, m).start()
        to_core(j, 0).start()
    for cp in xg:
        cp.wait_recv()

    def product(j, m):
        b = block(j, m)
        t, s = b // 4, b % 4
        to_core(j, m).wait_recv()
        return lax.dot_general(
            sd[s].reshape(512, 256), amp[b].reshape(256, 256), (((1,), (1,)), ((), ())), preferred_element_type=F32
        ), t

    for m in (0, 1, 3, 2):
        value, t = product(0, m) if m == 0 else (None, None)
        if m:
            to_y(0, m).wait_recv()
            to_core(0, m).start()
            value, t = product(0, m)
        dacc[t] = value

    for j in (1, 3, 2):
        for m in (0, 1, 3, 2):
            if m:
                to_y(j, m).wait_recv()
                to_core(j, m).start()
            value, t = product(j, m)
            if j == 2:
                d_ref[t] = (dacc[t] + value).astype(BF16)
            else:
                dacc[t] = dacc[t] + value

    @pl.loop(1, 32)
    def _(o):
        a_copy(o).wait_send()

    for p, q in first + second:
        p.wait_send()
        q.wait_send()
    for cp in zg + xg + fwd + [xch]:
        cp.wait_send()
    for q in (0, 1):
        hop(0, 8, q).wait_send()

        @pl.loop(1, 8)
        def _(d, q=q):
            hop(0, d, q).wait_send()
            hop(1, d, q).wait_send()

    for j in range(4):
        if j:
            to_z(j).wait_send()
        for m in range(4):
            if m:
                to_y(j, m).wait_send()
            to_core(j, m).wait_send()


def local(integrals, eps_occ, eps_vir, src_occ, occ_offset, vir_offset):
    x, y, z, c = coords()
    zh, zl = z // 4, z % 4
    ints = jnp.transpose(integrals, (1, 0, 2)).reshape(4, 4, 4, 32, 2, 128).transpose(0, 1, 2, 4, 3, 5)
    sources = jnp.stack([
        lax.dynamic_index_in_dim(integrals, src_occ[s], 1, keepdims=False) for s in range(4)
    ])
    vir = lax.dynamic_slice_in_dim(eps_vir, vir_offset[0], 256)
    vir_rows = lax.dynamic_slice_in_dim(vir, c * 128, 128)
    e_occ = lax.dynamic_index_in_dim(eps_occ, occ_offset[0] + (x * 4 + zh) * 4 + y, 0, keepdims=False)
    e_src = lax.dynamic_index_in_dim(
        eps_occ, occ_offset[0] + lax.dynamic_index_in_dim(src_occ, zl, 0, keepdims=False), 0, keepdims=False
    )
    denom = vir_rows[:, None] + vir[None, :] - e_occ - e_src
    vmem = pl.BlockSpec(memory_space=pltpu.VMEM)
    density = pl.pallas_call(
        kernel,
        out_shape=jax.ShapeDtypeStruct((4, 512, 256), BF16),
        in_specs=[vmem] * 3,
        out_specs=vmem,
        scratch_shapes=[
            pltpu.VMEM((4, 4, 4, 2, 32, 128), BF16),
            pltpu.VMEM((512, 1024), BF16),
            pltpu.VMEM((4, 4, 4, 2, 32, 256), BF16),
            pltpu.VMEM((4, 4, 4, 32, 256), BF16),
            pltpu.VMEM((16, 128, 256), F32),
            pltpu.VMEM((2, 8, 2, 64, 256), BF16),
            pltpu.VMEM((2, 8, 2, 64, 256), BF16),
            pltpu.VMEM((128, 256), BF16),
            pltpu.VMEM((128, 128), BF16),
            pltpu.VMEM((16, 2, 128, 256), BF16),
            pltpu.VMEM((4, 512, 256), F32),
            pltpu.SemaphoreType.DMA((COUNT,)),
            pltpu.SemaphoreType.DMA((COUNT,)),
        ],
        compiler_params=pltpu.CompilerParams(
            collective_id=0, has_side_effects=True, vmem_limit_bytes=48 << 20
        ),
        name="window",
    )(ints, sources, denom)
    return density.transpose(1, 0, 2)


def solution(mesh):
    in_specs = (P(("aux", "occ"), None, None), P(), P(), P(), P(), P())
    out_specs = P("aux", "occ", None)
    return jax.shard_map(local, mesh=mesh, in_specs=in_specs, out_specs=out_specs, check_vma=False)
```

```python
import jax
import jax.numpy as jnp
from jax import lax
from jax.experimental import pallas as pl
from jax.experimental.pallas import tpu as pltpu
from jax.sharding import PartitionSpec as P

MESH = pl.DeviceIdType.MESH
F32, BF16 = jnp.float32, jnp.bfloat16

Q = 4
SIZES = dict(A=96, SRC1=6, SRC2=6, FWD=8, ZG=4, XG=3, RING=16 * Q, AZ=3, AY=12, AR=8, AC=16, LOCAL=3)
SLOT, COUNT = {}, 0
for _name, _size in SIZES.items():
    SLOT[_name] = COUNT
    COUNT += _size
ORDER = (1, 3, 2)
CHUNKS = ((0, 1), (1, 3), (3, 4))


def coords():
    occ, aux = lax.axis_index("occ"), lax.axis_index("aux")
    return occ // 4, (aux // 2) % 4, (occ % 4) * 4 + aux // 8, aux % 2


def device(x, y, z, c):
    return {"occ": x * 4 + z // 4, "aux": ((z % 4) * 4 + y) * 2 + c}


def place(delta):
    low, high = delta % 2, delta // 2
    return 3 - 2 * low - 3 * high + 4 * low * high


def kernel(
    a_ref, eo_ref, ev_ref, so_ref, oo_ref, vo_ref, d_ref,
    arel, own_s, den, ar, at, sr, sd, cc, rb, sb, amp, dacc, snd, rcv,
):
    x, y, z, c = coords()
    zh, zl = z // 4, z % 4
    sends = []

    def copy(src, dst, slot, dev):
        return pltpu.make_async_remote_copy(
            src_ref=src, dst_ref=dst, send_sem=snd.at[slot], recv_sem=rcv.at[slot],
            device_id=dev, device_id_type=MESH,
        )

    def start(cp):
        cp.start()
        sends.append(cp)
        return cp

    barrier = pltpu.get_barrier_semaphore()

    def greet(dev):
        pl.semaphore_signal(barrier, inc=1, device_id=dev, device_id_type=MESH)

    greet(device(x, y, (z + 4) % 16, c))
    greet(device(x, y, (z + 12) % 16, c))

    @pl.loop(1, 32)
    def _(o):
        greet(device((x + o // 8) % 4, (y + (o // 2) % 4) % 4, z, (c + o) % 2))

    greet(device(x, y, (z + 1) % 16, c))
    greet(device(x, y, (z + 15) % 16, c))
    for j in ORDER:
        greet(device(x, y, zh * 4 + (zl + j) % 4, c))

    @pl.loop(0, 4)
    def _(tx):
        rows = a_ref[:, pl.ds(pl.multiple_of(tx * 16, 16), 16), :]
        turned = jnp.swapaxes(rows, 0, 1)
        for h in range(4):
            pos = place((h + 4 - zh) % 4)
            for ty in range(4):
                for tc in range(2):
                    arel[tx, pos, ty, tc] = turned[h * 4 + ty][:, tc * 128:(tc + 1) * 128]

    for s in range(4):
        j = so_ref[s]
        pos = place(((j // 4) % 4 + 4 - zh) % 4)
        for tc in range(2):
            own_s[s, :, tc * 128:(tc + 1) * 128] = arel[j // 16, pos, j % 4, tc]

    first_occ, first_vir = oo_ref[0], vo_ref[0]
    e_occ = eo_ref[first_occ + (x * 4 + zh) * 4 + y]
    e_src = eo_ref[first_occ + so_ref[zl]]
    row, lane = first_vir // 128, first_vir % 128
    window = jnp.concatenate(
        [ev_ref[pl.ds(row, 1), :], ev_ref[pl.ds(row + 1, 1), :], ev_ref[pl.ds(jnp.minimum(row + 2, 31), 1), :]], axis=1
    )

    def column(count, offset):
        at_lane = lax.broadcasted_iota(jnp.int32, (count, 384), 1)
        wanted = lax.broadcasted_iota(jnp.int32, (count, 384), 0) + offset
        return jnp.sum(jnp.where(at_lane == wanted, window, 0.0), axis=1, keepdims=True)

    whole = column(256, lane)
    diagonal = lax.broadcasted_iota(jnp.int32, (256, 256), 0) == lax.broadcasted_iota(jnp.int32, (256, 256), 1)
    vir_b = jnp.sum(jnp.where(diagonal, whole, 0.0), axis=0, keepdims=True)
    den[...] = column(128, lane + c * 128) + vir_b - e_occ - e_src

    pl.semaphore_wait(barrier, 38)

    local = [
        pltpu.make_async_copy(arel.at[x, :, y, c], ar.at[:, x, y, c], rcv.at[SLOT["LOCAL"]]),
        pltpu.make_async_copy(own_s, sr.at[:, x, y, c], rcv.at[SLOT["LOCAL"] + 1]),
        pltpu.make_async_copy(own_s, sd.at[:, x, zh], rcv.at[SLOT["LOCAL"] + 2]),
    ]
    for cp in local:
        cp.start()

    xs = {j: (x + j) % 4 for j in (1, 2, 3)}
    ys = {j: (y + j) % 4 for j in (1, 2, 3)}
    src1 = []
    for j in ORDER:
        src1.append(start(copy(own_s.at[0:2], sr.at[0:2, x, y, c], SLOT["SRC1"] + j - 1, device(xs[j], y, z, c))))
        src1.append(start(copy(own_s.at[2:4], sr.at[2:4, x, y, c], SLOT["SRC1"] + 2 + j, device(x, ys[j], z, c))))
    up4, down4 = device(x, y, (z + 4) % 16, c), device(x, y, (z + 12) % 16, c)
    zg = [
        start(copy(own_s, sd.at[:, x, zh], SLOT["ZG"], up4)),
        start(copy(own_s, sd.at[:, x, zh], SLOT["ZG"] + 1, down4)),
    ]

    def a_copy(o, chunk):
        lo, hi = CHUNKS[chunk]
        tx, ty, tc = (x + o // 8) % 4, (y + (o // 2) % 4) % 4, (c + o) % 2
        return copy(
            arel.at[tx, lo:hi, ty, tc], ar.at[lo:hi, x, y, c], SLOT["A"] + chunk * 32 + o, device(tx, ty, z, tc)
        )

    def a_each(chunk, act):
        @pl.loop(1, 32)
        def _(o):
            act(a_copy(o, chunk))

    a_each(0, lambda cp: cp.start())
    for cp in local:
        cp.wait()
    other = device(x, y, z, 1 - c)
    for cp in src1:
        cp.wait_recv()
    vx, vy = sr.at[0:2, :, y, c], sr.at[2:4, x, :, c]
    src2 = []
    for j in ORDER:
        src2.append(start(copy(vx, vx, SLOT["SRC2"] + j - 1, device(x, ys[j], z, c))))
        src2.append(start(copy(vy, vy, SLOT["SRC2"] + 2 + j, device(xs[j], y, z, c))))
    fwd = [start(copy(v, v, SLOT["FWD"] + n, other)) for n, v in enumerate((vx, vy))]
    a_each(1, lambda cp: cp.start())
    a_each(2, lambda cp: cp.start())
    for n, j in enumerate(ORDER):
        for k, view in enumerate((sr.at[0:2, :, (y + 4 - j) % 4, c], sr.at[2:4, (x + 4 - j) % 4, :, c])):
            src2[2 * n + k].wait_recv()
            fwd.append(start(copy(view, view, SLOT["FWD"] + 2 + 2 * n + k, other)))

    for k, cp in enumerate(list(zg)):
        cp.wait_recv()
        view = sd.at[0:2, x, (zh + 3) % 4] if k == 0 else sd.at[2:4, x, (zh + 1) % 4]
        zg.append(start(copy(view, view, SLOT["ZG"] + 2 + k, (up4, down4)[k])))

    def pairs(chunk, wait=()):
        lo, hi = CHUNKS[chunk]
        a_each(chunk, lambda cp: cp.wait_recv())
        for h in range(lo, hi):
            at[h * 128:(h + 1) * 128, :] = ar[h].reshape(1024, 128).T
        for cp in wait:
            cp.wait_recv()

        @pl.loop(0, 4)
        def _(s):
            part = jnp.dot(at[lo * 128:hi * 128, :], sr[s].reshape(1024, 256), preferred_element_type=F32)
            for h in range(lo, hi):
                cc[h * 4 + s] = part[(h - lo) * 128:(h - lo + 1) * 128]

    up, down = device(x, y, (z + 1) % 16, c), device(x, y, (z + 15) % 16, c)
    span = 128 // Q

    def hop(way, d, q):
        slot = SLOT["RING"] + (way * 8 + d - 1) * Q + q
        return copy(sb.at[way, d - 1, q], rb.at[way, d - 1, q], slot, up if way == 0 else down)

    def send(way, d, q, add):
        ahead = d if way == 0 else 16 - d
        target = (z + ahead) % 16
        spot = place((target // 4 + 4 - zh) % 4) * 4 + target % 4
        value = cc[spot, pl.ds(q * span, span), :]
        if add:
            hop(way, d + 1, q).wait_recv()
            value = value + rb[way, d, q].astype(F32)
        sb[way, d - 1, q] = value.astype(BF16)
        hop(way, d, q).start()

    def steps(lo, hi):
        @pl.loop(lo, hi)
        def _(k):
            for q in range(Q):
                send(0, 8 - k, q, True)
                send(1, 7 - k, q, True)

    def flush():
        for chunk in range(3):
            a_each(chunk, lambda cp: cp.wait_send())
        for cp in sends:
            cp.wait_send()

    def flush_ring():
        for q in range(Q):
            hop(0, 8, q).wait_send()

            @pl.loop(1, 8)
            def _(d, q=q):
                hop(0, d, q).wait_send()
                hop(1, d, q).wait_send()

    pairs(0, fwd)
    for q in range(Q):
        send(0, 8, q, False)
    pairs(1)
    for q in range(Q):
        send(1, 7, q, False)
    steps(1, 4)
    pairs(2)
    for cp in zg[2:]:
        cp.wait_recv()
    vd = sd.at[:, x]
    xg = [start(copy(vd, vd, SLOT["XG"] + j - 1, device(xs[j], y, z, c))) for j in ORDER]
    steps(4, 7)
    for q in range(Q):
        send(0, 1, q, True)

    own = amp.at[y * 4 + zl, c]
    mine = place(0) * 4 + zl
    for q in range(Q):
        rows = pl.ds(q * span, span)
        hop(1, 1, q).wait_recv()
        total = cc[mine, rows, :] + rb[1, 0, q].astype(F32)
        hop(0, 1, q).wait_recv()
        total = total + rb[0, 0, q].astype(F32)
        own[rows, :] = (total / den[rows, :]).astype(BF16)

    def block(j, m):
        return (y + 4 - m) % 4 * 4 + (zl + 4 - j) % 4

    def to_z(j):
        return copy(own, own, SLOT["AZ"] + j - 1, device(x, y, zh * 4 + (zl + j) % 4, c))

    def to_y(j, m):
        view = amp.at[block(j, 0), c]
        return copy(view, view, SLOT["AY"] + j * 3 + m - 1, device(x, ys[m], z, c))

    def relay(j, half):
        view = amp.at[block(j, (1, 3)[half]), c, half * 64:(half + 1) * 64]
        return copy(view, view, SLOT["AR"] + j * 2 + half, device(x, ys[(1, 3)[half]], z, c))

    def to_core(j, m):
        view = amp.at[block(j, m), c]
        return copy(view, view, SLOT["AC"] + j * 4 + m, other)

    touched = set()

    def product(j, m, last=False):
        to_core(j, m).wait_recv()
        b = block(j, m)
        t, s = b // 4, b % 4
        lhs, rhs = sd[s].reshape(512, 256), amp[b].reshape(256, 256)
        straight = lax.dot_general(lhs, rhs, (((1,), (1,)), ((), ())), preferred_element_type=F32)
        crossed = jnp.dot(lhs, rhs, preferred_element_type=F32)
        value = 2.0 * straight - crossed
        if m in touched:
            value = dacc[t] + value
        touched.add(m)
        if last:
            d_ref[t] = value.astype(BF16)
        else:
            dacc[t] = value

    turn = (0, 1, 3, 2)
    for j in turn:
        if j:
            to_z(j).wait_recv()
        start(to_y(j, 1))
        start(to_y(j, 3))
        if not j:
            for k in ORDER:
                start(to_z(k))
        start(to_core(j, 0))
    for cp in xg:
        cp.wait_recv()
    for n, j in enumerate(turn):
        for half, m in enumerate((1, 3)):
            to_y(j, m).wait_recv()
            start(relay(j, half))
            start(to_core(j, m))
        if n:
            for m in (0, 1, 3):
                product(turn[n - 1], m)
    for n, j in enumerate(turn):
        for half in range(2):
            relay(j, half).wait_recv()
        start(to_core(j, 2))
        if n == 0:
            for m in (0, 1, 3):
                product(turn[3], m, True)
        else:
            product(turn[n - 1], 2)
    product(turn[3], 2, True)
    flush()
    flush_ring()


def window(integrals, eps_occ, eps_vir, src_occ, occ_offset, vir_offset):
    vmem, smem = pl.BlockSpec(memory_space=pltpu.VMEM), pl.BlockSpec(memory_space=pltpu.SMEM)
    return pl.pallas_call(
        kernel,
        out_shape=jax.ShapeDtypeStruct((4, 512, 256), BF16),
        in_specs=[vmem, smem, vmem, smem, smem, smem],
        out_specs=vmem,
        scratch_shapes=[
            pltpu.VMEM((4, 4, 4, 2, 32, 128), BF16),
            pltpu.VMEM((4, 32, 256), BF16),
            pltpu.VMEM((128, 256), F32),
            pltpu.VMEM((4, 4, 4, 2, 32, 128), BF16),
            pltpu.VMEM((512, 1024), BF16),
            pltpu.VMEM((4, 4, 4, 2, 32, 256), BF16),
            pltpu.VMEM((4, 4, 4, 32, 256), BF16),
            pltpu.VMEM((16, 128, 256), F32),
            pltpu.VMEM((2, 8, Q, 128 // Q, 256), BF16),
            pltpu.VMEM((2, 8, Q, 128 // Q, 256), BF16),
            pltpu.VMEM((16, 2, 128, 256), BF16),
            pltpu.VMEM((4, 512, 256), F32),
            pltpu.SemaphoreType.DMA((COUNT,)),
            pltpu.SemaphoreType.DMA((COUNT,)),
        ],
        compiler_params=pltpu.CompilerParams(
            collective_id=0, has_side_effects=True, vmem_limit_bytes=48 << 20
        ),
        name="window",
    )(integrals, eps_occ, eps_vir.reshape(32, 128), src_occ, occ_offset, vir_offset)


def local(*args):
    return window(*args).transpose(1, 0, 2)


def solution(mesh):
    in_specs = (P(("aux", "occ"), None, None), P(), P(), P(), P(), P())
    out_specs = P("aux", "occ", None)
    return jax.shard_map(local, mesh=mesh, in_specs=in_specs, out_specs=out_specs, check_vma=False)
```

```python
import jax
import jax.numpy as jnp
from jax import lax
from jax.experimental import pallas as pl
from jax.experimental.pallas import tpu as pltpu
from jax.sharding import PartitionSpec as P

MESH = pl.DeviceIdType.MESH
F32, BF16 = jnp.float32, jnp.bfloat16

Q = 4
SIZES = dict(A=128, SRC1=6, SRC2=6, FWD=8, ZG=4, XG=3, RING=16 * Q, AZ=6, AY=24, AR=8, AC=32, LOCAL=3, LOAD=6)
SLOT, COUNT = {}, 0
for _name, _size in SIZES.items():
    SLOT[_name] = COUNT
    COUNT += _size
ORDER = (1, 3, 2)
CHUNKS = ((0, 1), (1, 2), (2, 3), (3, 4))


def coords():
    occ, aux = lax.axis_index("occ"), lax.axis_index("aux")
    return occ // 4, (aux // 2) % 4, (occ % 4) * 4 + aux // 8, aux % 2


def device(x, y, z, c):
    return {"occ": x * 4 + z // 4, "aux": ((z % 4) * 4 + y) * 2 + c}


def place(delta):
    low, high = delta % 2, delta // 2
    return 3 - 2 * low - 3 * high + 4 * low * high


def kernel(
    a_hbm, eo_hbm, ev_hbm, so_hbm, oo_hbm, vo_hbm, d_ref,
    a_ref, eo_ref, ev_ref, so_ref, oo_ref, vo_ref,
    arel, own_s, den, ar, at, sr, sd, cc, rb, sb, amp, dacc, snd, rcv,
):
    x, y, z, c = coords()
    zh, zl = z // 4, z % 4
    sends = []

    def copy(src, dst, slot, dev):
        return pltpu.make_async_remote_copy(
            src_ref=src, dst_ref=dst, send_sem=snd.at[slot], recv_sem=rcv.at[slot],
            device_id=dev, device_id_type=MESH,
        )

    def start(cp):
        cp.start()
        sends.append(cp)
        return cp

    loads = [
        pltpu.make_async_copy(src, dst, rcv.at[SLOT["LOAD"] + n])
        for n, (src, dst) in enumerate((
            (so_hbm, so_ref), (a_hbm, a_ref), (oo_hbm, oo_ref), (vo_hbm, vo_ref), (eo_hbm, eo_ref), (ev_hbm, ev_ref),
        ))
    ]
    for cp in loads:
        cp.start()
    barrier = pltpu.get_barrier_semaphore()

    def greet(dev):
        pl.semaphore_signal(barrier, inc=1, device_id=dev, device_id_type=MESH)

    greet(device(x, y, (z + 4) % 16, c))
    greet(device(x, y, (z + 12) % 16, c))

    @pl.loop(1, 32)
    def _(o):
        greet(device((x + o // 8) % 4, (y + (o // 2) % 4) % 4, z, (c + o) % 2))

    greet(device(x, y, (z + 1) % 16, c))
    greet(device(x, y, (z + 15) % 16, c))
    for j in ORDER:
        greet(device(x, y, zh * 4 + (zl + j) % 4, c))

    for cp in loads:
        cp.wait()
    row16 = lax.broadcasted_iota(jnp.int32, (16, 16, 256), 1)

    @pl.loop(0, 2)
    def _(p):
        lines = pl.ds(pl.multiple_of(p * 16, 16), 16)
        found = [jnp.zeros((16, 256), F32)] * 4
        for g in range(4):
            rows = a_ref[lines, g * 16:(g + 1) * 16, :].astype(F32)
            found = [
                found[s] + jnp.sum(jnp.where(row16 == so_ref[s] - g * 16, rows, 0.0), axis=1) for s in range(4)
            ]
        for s in range(4):
            own_s[s, lines, :] = found[s].astype(BF16)

    pl.semaphore_wait(barrier, 38)

    local = [
        pltpu.make_async_copy(own_s, sr.at[:, x, y, c], rcv.at[SLOT["LOCAL"] + 1]),
        pltpu.make_async_copy(own_s, sd.at[:, x, zh], rcv.at[SLOT["LOCAL"] + 2]),
    ]
    for cp in local:
        cp.start()

    xs = {j: (x + j) % 4 for j in (1, 2, 3)}
    ys = {j: (y + j) % 4 for j in (1, 2, 3)}
    src1 = []
    for j in ORDER:
        src1.append(start(copy(own_s.at[0:2], sr.at[0:2, x, y, c], SLOT["SRC1"] + j - 1, device(xs[j], y, z, c))))
        src1.append(start(copy(own_s.at[2:4], sr.at[2:4, x, y, c], SLOT["SRC1"] + 2 + j, device(x, ys[j], z, c))))
    up4, down4 = device(x, y, (z + 4) % 16, c), device(x, y, (z + 12) % 16, c)
    zg = [
        start(copy(own_s, sd.at[:, x, zh], SLOT["ZG"], up4)),
        start(copy(own_s, sd.at[:, x, zh], SLOT["ZG"] + 1, down4)),
    ]

    def a_copy(o, chunk):
        lo, hi = CHUNKS[chunk]
        tx, ty, tc = (x + o // 8) % 4, (y + (o // 2) % 4) % 4, (c + o) % 2
        return copy(
            arel.at[tx, lo:hi, ty, tc], ar.at[lo:hi, x, y, c], SLOT["A"] + chunk * 32 + o, device(tx, ty, z, tc)
        )

    def a_each(chunk, act):
        @pl.loop(1, 32)
        def _(o):
            act(a_copy(o, chunk))

    @pl.loop(0, 4)
    def _(tx):
        rows = a_ref[:, pl.ds(pl.multiple_of(tx * 16, 16), 16), :]
        turned = jnp.swapaxes(rows, 0, 1)
        for h in range(4):
            pos = place((h + 4 - zh) % 4)
            for ty in range(4):
                for tc in range(2):
                    arel[tx, pos, ty, tc] = turned[h * 4 + ty][:, tc * 128:(tc + 1) * 128]

    keep = pltpu.make_async_copy(arel.at[x, :, y, c], ar.at[:, x, y, c], rcv.at[SLOT["LOCAL"]])
    keep.start()
    for cp in local:
        cp.wait()
    other = device(x, y, z, 1 - c)
    for cp in src1:
        cp.wait_recv()
    vx, vy = sr.at[0:2, :, y, c], sr.at[2:4, x, :, c]
    src2 = []
    for j in ORDER:
        src2.append(start(copy(vx, vx, SLOT["SRC2"] + j - 1, device(x, ys[j], z, c))))
        src2.append(start(copy(vy, vy, SLOT["SRC2"] + 2 + j, device(xs[j], y, z, c))))
    fwd = [start(copy(v, v, SLOT["FWD"] + n, other)) for n, v in enumerate((vx, vy))]
    for chunk in range(4):
        a_each(chunk, lambda cp: cp.start())
    first_occ, first_vir = oo_ref[0], vo_ref[0]
    at_occ = lax.broadcasted_iota(jnp.int32, (8, 128), 0) * 128 + lax.broadcasted_iota(jnp.int32, (8, 128), 1)

    def occupied(index):
        kept = jnp.where(at_occ == first_occ + index, eo_ref[...], 0.0)
        return jnp.sum(jnp.sum(kept, axis=1, keepdims=True), axis=0, keepdims=True)

    e_occ = occupied((x * 4 + zh) * 4 + y)
    e_src = occupied(so_ref[zl])
    row, lane = first_vir // 128, first_vir % 128
    at_row = lax.broadcasted_iota(jnp.int32, (32, 128), 0)
    window = jnp.concatenate(
        [jnp.sum(jnp.where(at_row == row + n, ev_ref[...], 0.0), axis=0, keepdims=True) for n in range(3)], axis=1
    )

    def column(count, offset):
        at_lane = lax.broadcasted_iota(jnp.int32, (count, 384), 1)
        wanted = lax.broadcasted_iota(jnp.int32, (count, 384), 0) + offset
        return jnp.sum(jnp.where(at_lane == wanted, window, 0.0), axis=1, keepdims=True)

    whole = column(256, lane)
    diagonal = lax.broadcasted_iota(jnp.int32, (256, 256), 0) == lax.broadcasted_iota(jnp.int32, (256, 256), 1)
    vir_b = jnp.sum(jnp.where(diagonal, whole, 0.0), axis=0, keepdims=True)
    den[...] = column(128, lane + c * 128) + vir_b - e_occ - e_src

    keep.wait()
    for n, j in enumerate(ORDER):
        for k, view in enumerate((sr.at[0:2, :, (y + 4 - j) % 4, c], sr.at[2:4, (x + 4 - j) % 4, :, c])):
            src2[2 * n + k].wait_recv()
            fwd.append(start(copy(view, view, SLOT["FWD"] + 2 + 2 * n + k, other)))

    for k, cp in enumerate(list(zg)):
        cp.wait_recv()
        view = sd.at[0:2, x, (zh + 3) % 4] if k == 0 else sd.at[2:4, x, (zh + 1) % 4]
        zg.append(start(copy(view, view, SLOT["ZG"] + 2 + k, (up4, down4)[k])))

    def turn_over(chunk):
        a_each(chunk, lambda cp: cp.wait_recv())
        at[chunk * 128:(chunk + 1) * 128, :] = ar[chunk].reshape(1024, 128).T

    def pairs(lo, hi):
        @pl.loop(0, 4)
        def _(s):
            part = jnp.dot(at[lo * 128:hi * 128, :], sr[s].reshape(1024, 256), preferred_element_type=F32)
            for h in range(lo, hi):
                cc[h * 4 + s] = part[(h - lo) * 128:(h - lo + 1) * 128]

    up, down = device(x, y, (z + 1) % 16, c), device(x, y, (z + 15) % 16, c)
    span = 128 // Q

    def hop(way, d, q):
        slot = SLOT["RING"] + (way * 8 + d - 1) * Q + q
        return copy(sb.at[way, d - 1, q], rb.at[way, d - 1, q], slot, up if way == 0 else down)

    def send(way, d, q, add):
        ahead = d if way == 0 else 16 - d
        target = (z + ahead) % 16
        spot = place((target // 4 + 4 - zh) % 4) * 4 + target % 4
        value = cc[spot, pl.ds(q * span, span), :]
        if add:
            hop(way, d + 1, q).wait_recv()
            value = value + rb[way, d, q].astype(F32)
        sb[way, d - 1, q] = value.astype(BF16)
        hop(way, d, q).start()

    def steps(lo, hi):
        @pl.loop(lo, hi)
        def _(k):
            for q in range(Q):
                send(0, 8 - k, q, True)
                send(1, 7 - k, q, True)

    def flush():
        for chunk in range(4):
            a_each(chunk, lambda cp: cp.wait_send())
        for cp in sends:
            cp.wait_send()

    def flush_ring():
        for q in range(Q):
            hop(0, 8, q).wait_send()

            @pl.loop(1, 8)
            def _(d, q=q):
                hop(0, d, q).wait_send()
                hop(1, d, q).wait_send()

    turn_over(0)
    for cp in fwd:
        cp.wait_recv()
    pairs(0, 1)
    for q in range(Q):
        send(0, 8, q, False)
    turn_over(1)
    turn_over(2)
    pairs(1, 3)
    for q in range(Q):
        send(1, 7, q, False)
    steps(1, 4)
    turn_over(3)
    pairs(3, 4)
    for cp in zg[2:]:
        cp.wait_recv()
    vd = sd.at[:, x]
    xg = [start(copy(vd, vd, SLOT["XG"] + j - 1, device(xs[j], y, z, c))) for j in ORDER]
    steps(4, 7)
    for q in range(Q):
        send(0, 1, q, True)

    mine = place(0) * 4 + zl
    part = (pl.ds(0, 64), pl.ds(64, 64))

    def block(j, m):
        return (y + 4 - m) % 4 * 4 + (zl + 4 - j) % 4

    def to_z(j, h):
        view = amp.at[block(0, 0), c, part[h]]
        return copy(view, view, SLOT["AZ"] + (j - 1) * 2 + h, device(x, y, zh * 4 + (zl + j) % 4, c))

    def to_y(j, m, h):
        view = amp.at[block(j, 0), c, part[h]]
        return copy(view, view, SLOT["AY"] + (j * 3 + m - 1) * 2 + h, device(x, ys[m], z, c))

    def relay(j, h):
        view = amp.at[block(j, (1, 3)[h]), c, part[h]]
        return copy(view, view, SLOT["AR"] + j * 2 + h, device(x, ys[(1, 3)[h]], z, c))

    def to_core(j, m, h):
        view = amp.at[block(j, m), c, part[h]]
        return copy(view, view, SLOT["AC"] + (j * 4 + m) * 2 + h, other)

    def spread(j, h):
        if j == 0:
            for k in (2, 1, 3):
                start(to_z(k, h))
        start(to_y(j, 1, h))
        start(to_y(j, 3, h))
        start(to_core(j, 0, h))

    for q in range(Q):
        rows = pl.ds(q * span, span)
        hop(1, 1, q).wait_recv()
        total = cc[mine, rows, :] + rb[1, 0, q].astype(F32)
        hop(0, 1, q).wait_recv()
        total = total + rb[0, 0, q].astype(F32)
        amp[block(0, 0), c, rows, :] = (total / den[rows, :]).astype(BF16)
        if (q + 1) * span % 64 == 0:
            spread(0, (q + 1) * span // 64 - 1)

    touched = set()

    def product(j, m, last=False):
        for h in range(2):
            to_core(j, m, h).wait_recv()
        b = block(j, m)
        t, s = b // 4, b % 4
        lhs, rhs = sd[s].reshape(512, 256), amp[b].reshape(256, 256)
        straight = lax.dot_general(lhs, rhs, (((1,), (1,)), ((), ())), preferred_element_type=F32)
        crossed = jnp.dot(lhs, rhs, preferred_element_type=F32)
        value = 2.0 * straight - crossed
        if m in touched:
            value = dacc[t] + value
        touched.add(m)
        if last:
            d_ref[t] = value.astype(BF16)
        else:
            dacc[t] = value

    turn = (0, 1, 3, 2)

    def pass_on(j):
        for h in range(2):
            for m in (1, 3):
                to_y(j, m, h).wait_recv()
                if m == (1, 3)[h]:
                    start(relay(j, h))
                start(to_core(j, m, h))

    for j in turn[1:]:
        for h in range(2):
            to_z(j, h).wait_recv()
            spread(j, h)
    for j in turn:
        pass_on(j)
    for cp in xg:
        cp.wait_recv()
    for j in turn[:3]:
        for m in (0, 1, 3):
            product(j, m)

    def take(j):
        for h in range(2):
            relay(j, h).wait_recv()
            start(to_core(j, 2, h))

    for j in turn:
        take(j)
    for m in (0, 1, 3):
        product(turn[3], m, True)
    for j in turn:
        product(j, 2, j == turn[3])
    flush()
    flush_ring()


def window(integrals, eps_occ, eps_vir, src_occ, occ_offset, vir_offset):
    return pl.pallas_call(
        kernel,
        out_shape=jax.ShapeDtypeStruct((4, 512, 256), BF16),
        in_specs=[pl.BlockSpec(memory_space=pl.ANY)] * 6,
        out_specs=pl.BlockSpec(memory_space=pltpu.VMEM),
        scratch_shapes=[
            pltpu.VMEM((32, 64, 256), BF16),
            pltpu.VMEM((8, 128), F32),
            pltpu.VMEM((32, 128), F32),
            pltpu.SMEM((4,), jnp.int32),
            pltpu.SMEM((1,), jnp.int32),
            pltpu.SMEM((1,), jnp.int32),
            pltpu.VMEM((4, 4, 4, 2, 32, 128), BF16),
            pltpu.VMEM((4, 32, 256), BF16),
            pltpu.VMEM((128, 256), F32),
            pltpu.VMEM((4, 4, 4, 2, 32, 128), BF16),
            pltpu.VMEM((512, 1024), BF16),
            pltpu.VMEM((4, 4, 4, 2, 32, 256), BF16),
            pltpu.VMEM((4, 4, 4, 32, 256), BF16),
            pltpu.VMEM((16, 128, 256), F32),
            pltpu.VMEM((2, 8, Q, 128 // Q, 256), BF16),
            pltpu.VMEM((2, 8, Q, 128 // Q, 256), BF16),
            pltpu.VMEM((16, 2, 128, 256), BF16),
            pltpu.VMEM((4, 512, 256), F32),
            pltpu.SemaphoreType.DMA((COUNT,)),
            pltpu.SemaphoreType.DMA((COUNT,)),
        ],
        compiler_params=pltpu.CompilerParams(
            collective_id=0, has_side_effects=True, vmem_limit_bytes=66 * 10**6
        ),
        name="window",
    )(integrals, eps_occ.reshape(8, 128), eps_vir.reshape(32, 128), src_occ, occ_offset, vir_offset)


def local(*args):
    return window(*args).transpose(1, 0, 2)


def solution(mesh):
    in_specs = (P(("aux", "occ"), None, None), P(), P(), P(), P(), P())
    out_specs = P("aux", "occ", None)
    return jax.shard_map(local, mesh=mesh, in_specs=in_specs, out_specs=out_specs, check_vma=False)
```

```python
import jax
import jax.numpy as jnp
from jax import lax
from jax.experimental import pallas as pl
from jax.experimental.pallas import tpu as pltpu
from jax.sharding import PartitionSpec as P

MESH = pl.DeviceIdType.MESH
F32, BF16 = jnp.float32, jnp.bfloat16

Q = 4
SIZES = dict(A=128, SRC1=6, SRC2=6, FWD=8, ZG=4, XG=3, RING=16 * Q, AZ=6, AY=24, AR=8, AC=32, LOCAL=3, LOAD=6)
SLOT, COUNT = {}, 0
for _name, _size in SIZES.items():
    SLOT[_name] = COUNT
    COUNT += _size
ORDER = (1, 3, 2)
CHUNKS = ((0, 1), (1, 3), (3, 4))


def coords():
    occ, aux = lax.axis_index("occ"), lax.axis_index("aux")
    return occ // 4, (aux // 2) % 4, (occ % 4) * 4 + aux // 8, aux % 2


def device(x, y, z, c):
    return {"occ": x * 4 + z // 4, "aux": ((z % 4) * 4 + y) * 2 + c}


def place(delta):
    low, high = delta % 2, delta // 2
    return 3 - 2 * low - 3 * high + 4 * low * high


def kernel(
    a_hbm, eo_hbm, ev_hbm, so_ref, oo_ref, vo_ref, d_ref, a_ref, eo_ref, ev_ref,
    arel, own_s, den, ar, at, sr, sd, cc, rb, sb, amp, dacc, snd, rcv,
):
    x, y, z, c = coords()
    zh, zl = z // 4, z % 4
    sends = []

    def copy(src, dst, slot, dev):
        return pltpu.make_async_remote_copy(
            src_ref=src, dst_ref=dst, send_sem=snd.at[slot], recv_sem=rcv.at[slot],
            device_id=dev, device_id_type=MESH,
        )

    def start(cp):
        cp.start()
        sends.append(cp)
        return cp

    loads = [
        pltpu.make_async_copy(src, dst, rcv.at[SLOT["LOAD"] + n])
        for n, (src, dst) in enumerate((
            (a_hbm, a_ref), (eo_hbm, eo_ref), (ev_hbm, ev_ref),
        ))
    ]
    for cp in loads:
        cp.start()
    barrier = pltpu.get_barrier_semaphore()

    def greet(dev):
        pl.semaphore_signal(barrier, inc=1, device_id=dev, device_id_type=MESH)

    greet(device(x, y, (z + 4) % 16, c))
    greet(device(x, y, (z + 12) % 16, c))

    @pl.loop(1, 32)
    def _(o):
        greet(device((x + o // 8) % 4, (y + (o // 2) % 4) % 4, z, (c + o) % 2))

    greet(device(x, y, (z + 1) % 16, c))
    greet(device(x, y, (z + 15) % 16, c))
    for j in ORDER:
        greet(device(x, y, zh * 4 + (zl + j) % 4, c))

    for cp in loads[:1]:
        cp.wait()
    @pl.loop(0, 4)
    def _(tx):
        rows = a_ref[:, pl.ds(pl.multiple_of(tx * 16, 16), 16), :]
        turned = jnp.swapaxes(rows, 0, 1)
        for h in range(4):
            pos = place((h + 4 - zh) % 4)
            for ty in range(4):
                for tc in range(2):
                    arel[tx, pos, ty, tc] = turned[h * 4 + ty][:, tc * 128:(tc + 1) * 128]

    for s in range(4):
        j = so_ref[s]
        pos = place(((j // 4) % 4 + 4 - zh) % 4)
        for tc in range(2):
            own_s[s, :, tc * 128:(tc + 1) * 128] = arel[j // 16, pos, j % 4, tc]

    pl.semaphore_wait(barrier, 38)

    local = [
        pltpu.make_async_copy(own_s, sr.at[:, x, y, c], rcv.at[SLOT["LOCAL"] + 1]),
        pltpu.make_async_copy(own_s, sd.at[:, x, zh], rcv.at[SLOT["LOCAL"] + 2]),
    ]
    for cp in local:
        cp.start()

    xs = {j: (x + j) % 4 for j in (1, 2, 3)}
    ys = {j: (y + j) % 4 for j in (1, 2, 3)}
    src1 = []
    for j in ORDER:
        src1.append(start(copy(own_s.at[0:2], sr.at[0:2, x, y, c], SLOT["SRC1"] + j - 1, device(xs[j], y, z, c))))
        src1.append(start(copy(own_s.at[2:4], sr.at[2:4, x, y, c], SLOT["SRC1"] + 2 + j, device(x, ys[j], z, c))))
    up4, down4 = device(x, y, (z + 4) % 16, c), device(x, y, (z + 12) % 16, c)
    zg = [
        start(copy(own_s, sd.at[:, x, zh], SLOT["ZG"], up4)),
        start(copy(own_s, sd.at[:, x, zh], SLOT["ZG"] + 1, down4)),
    ]

    def a_copy(o, chunk):
        lo, hi = CHUNKS[chunk]
        tx, ty, tc = (x + o // 8) % 4, (y + (o // 2) % 4) % 4, (c + o) % 2
        return copy(
            arel.at[tx, lo:hi, ty, tc], ar.at[lo:hi, x, y, c], SLOT["A"] + chunk * 32 + o, device(tx, ty, z, tc)
        )

    def a_each(chunk, act):
        @pl.loop(1, 32)
        def _(o):
            act(a_copy(o, chunk))

    keep = pltpu.make_async_copy(arel.at[x, :, y, c], ar.at[:, x, y, c], rcv.at[SLOT["LOCAL"]])
    keep.start()
    for cp in local:
        cp.wait()
    other = device(x, y, z, 1 - c)
    for cp in src1:
        cp.wait_recv()
    vx, vy = sr.at[0:2, :, y, c], sr.at[2:4, x, :, c]
    src2 = []
    for j in ORDER:
        src2.append(start(copy(vx, vx, SLOT["SRC2"] + j - 1, device(x, ys[j], z, c))))
        src2.append(start(copy(vy, vy, SLOT["SRC2"] + 2 + j, device(xs[j], y, z, c))))
    fwd = [start(copy(v, v, SLOT["FWD"] + n, other)) for n, v in enumerate((vx, vy))]
    for chunk in range(3):
        a_each(chunk, lambda cp: cp.start())
    for cp in loads[1:]:
        cp.wait()
    first_occ, first_vir = oo_ref[0], vo_ref[0]
    at_occ = lax.broadcasted_iota(jnp.int32, (8, 128), 0) * 128 + lax.broadcasted_iota(jnp.int32, (8, 128), 1)

    def occupied(index):
        kept = jnp.where(at_occ == first_occ + index, eo_ref[...], 0.0)
        return jnp.sum(jnp.sum(kept, axis=1, keepdims=True), axis=0, keepdims=True)

    e_occ = occupied((x * 4 + zh) * 4 + y)
    e_src = occupied(so_ref[zl])
    row, lane = first_vir // 128, first_vir % 128
    at_row = lax.broadcasted_iota(jnp.int32, (32, 128), 0)
    window = jnp.concatenate(
        [jnp.sum(jnp.where(at_row == row + n, ev_ref[...], 0.0), axis=0, keepdims=True) for n in range(3)], axis=1
    )

    def column(count, offset):
        at_lane = lax.broadcasted_iota(jnp.int32, (count, 384), 1)
        wanted = lax.broadcasted_iota(jnp.int32, (count, 384), 0) + offset
        return jnp.sum(jnp.where(at_lane == wanted, window, 0.0), axis=1, keepdims=True)

    whole = column(256, lane)
    diagonal = lax.broadcasted_iota(jnp.int32, (256, 256), 0) == lax.broadcasted_iota(jnp.int32, (256, 256), 1)
    vir_b = jnp.sum(jnp.where(diagonal, whole, 0.0), axis=0, keepdims=True)
    den[...] = column(128, lane + c * 128) + vir_b - e_occ - e_src

    keep.wait()
    for n, j in enumerate(ORDER):
        for k, view in enumerate((sr.at[0:2, :, (y + 4 - j) % 4, c], sr.at[2:4, (x + 4 - j) % 4, :, c])):
            src2[2 * n + k].wait_recv()
            fwd.append(start(copy(view, view, SLOT["FWD"] + 2 + 2 * n + k, other)))

    for k, cp in enumerate(list(zg)):
        cp.wait_recv()
        view = sd.at[0:2, x, (zh + 3) % 4] if k == 0 else sd.at[2:4, x, (zh + 1) % 4]
        zg.append(start(copy(view, view, SLOT["ZG"] + 2 + k, (up4, down4)[k])))

    def turn_over(chunk):
        a_each(chunk, lambda cp: cp.wait_recv())
        for h in range(*CHUNKS[chunk]):
            at[h * 128:(h + 1) * 128, :] = ar[h].reshape(1024, 128).T

    def pairs(lo, hi):
        @pl.loop(0, 4)
        def _(s):
            part = jnp.dot(at[lo * 128:hi * 128, :], sr[s].reshape(1024, 256), preferred_element_type=F32)
            for h in range(lo, hi):
                cc[h * 4 + s] = part[(h - lo) * 128:(h - lo + 1) * 128]

    up, down = device(x, y, (z + 1) % 16, c), device(x, y, (z + 15) % 16, c)
    span = 128 // Q

    def hop(way, d, q):
        slot = SLOT["RING"] + (way * 8 + d - 1) * Q + q
        return copy(sb.at[way, d - 1, q], rb.at[way, d - 1, q], slot, up if way == 0 else down)

    def send(way, d, q, add):
        ahead = d if way == 0 else 16 - d
        target = (z + ahead) % 16
        spot = place((target // 4 + 4 - zh) % 4) * 4 + target % 4
        value = cc[spot, pl.ds(q * span, span), :]
        if add:
            hop(way, d + 1, q).wait_recv()
            value = value + rb[way, d, q].astype(F32)
        sb[way, d - 1, q] = value.astype(BF16)
        hop(way, d, q).start()

    def steps(lo, hi):
        @pl.loop(lo, hi)
        def _(k):
            for q in range(Q):
                send(0, 8 - k, q, True)
                send(1, 7 - k, q, True)

    def flush():
        for chunk in range(3):
            a_each(chunk, lambda cp: cp.wait_send())
        for cp in sends:
            cp.wait_send()

    def flush_ring():
        for q in range(Q):
            hop(0, 8, q).wait_send()

            @pl.loop(1, 8)
            def _(d, q=q):
                hop(0, d, q).wait_send()
                hop(1, d, q).wait_send()

    turn_over(0)
    for cp in fwd:
        cp.wait_recv()
    pairs(0, 1)
    for q in range(Q):
        send(0, 8, q, False)
    turn_over(1)
    pairs(1, 3)
    for q in range(Q):
        send(1, 7, q, False)
    steps(1, 4)
    turn_over(2)
    pairs(3, 4)
    for cp in zg[2:]:
        cp.wait_recv()
    vd = sd.at[:, x]
    xg = [start(copy(vd, vd, SLOT["XG"] + j - 1, device(xs[j], y, z, c))) for j in ORDER]
    steps(4, 7)
    for q in range(Q):
        send(0, 1, q, True)

    mine = place(0) * 4 + zl
    part = (pl.ds(0, 64), pl.ds(64, 64))

    def block(j, m):
        return (y + 4 - m) % 4 * 4 + (zl + 4 - j) % 4

    def to_z(j, h):
        view = amp.at[block(0, 0), c, part[h]]
        return copy(view, view, SLOT["AZ"] + (j - 1) * 2 + h, device(x, y, zh * 4 + (zl + j) % 4, c))

    def to_y(j, m, h):
        view = amp.at[block(j, 0), c, part[h]]
        return copy(view, view, SLOT["AY"] + (j * 3 + m - 1) * 2 + h, device(x, ys[m], z, c))

    def relay(j, h):
        view = amp.at[block(j, (1, 3)[h]), c, part[h]]
        return copy(view, view, SLOT["AR"] + j * 2 + h, device(x, ys[(1, 3)[h]], z, c))

    def to_core(j, m, h):
        view = amp.at[block(j, m), c, part[h]]
        return copy(view, view, SLOT["AC"] + (j * 4 + m) * 2 + h, other)

    def spread(j, h):
        if j == 0:
            for k in (2, 1, 3):
                start(to_z(k, h))
        start(to_y(j, 1, h))
        start(to_y(j, 3, h))
        start(to_core(j, 0, h))

    for q in range(Q):
        rows = pl.ds(q * span, span)
        hop(1, 1, q).wait_recv()
        total = cc[mine, rows, :] + rb[1, 0, q].astype(F32)
        hop(0, 1, q).wait_recv()
        total = total + rb[0, 0, q].astype(F32)
        amp[block(0, 0), c, rows, :] = (total / den[rows, :]).astype(BF16)
        if (q + 1) * span % 64 == 0:
            spread(0, (q + 1) * span // 64 - 1)

    touched = set()

    def product(j, m, last=False):
        for h in range(2):
            to_core(j, m, h).wait_recv()
        b = block(j, m)
        t, s = b // 4, b % 4
        lhs, rhs = sd[s].reshape(512, 256), amp[b].reshape(256, 256)
        straight = lax.dot_general(lhs, rhs, (((1,), (1,)), ((), ())), preferred_element_type=F32)
        crossed = jnp.dot(lhs, rhs, preferred_element_type=F32)
        value = 2.0 * straight - crossed
        if m in touched:
            value = dacc[t] + value
        touched.add(m)
        if last:
            d_ref[t] = value.astype(BF16)
        else:
            dacc[t] = value

    turn = (0, 1, 3, 2)

    def pass_on(j):
        for h in range(2):
            for m in (1, 3):
                to_y(j, m, h).wait_recv()
                if m == (1, 3)[h]:
                    start(relay(j, h))
                start(to_core(j, m, h))

    for j in turn[1:]:
        for h in range(2):
            to_z(j, h).wait_recv()
            spread(j, h)
    for j in turn:
        pass_on(j)
    for cp in xg:
        cp.wait_recv()
    for j in turn[:3]:
        for m in (0, 1, 3):
            product(j, m)

    def take(j):
        for h in range(2):
            relay(j, h).wait_recv()
            start(to_core(j, 2, h))

    for j in turn:
        take(j)
    for m in (0, 1, 3):
        product(turn[3], m, True)
    for j in turn:
        product(j, 2, j == turn[3])
    flush()
    flush_ring()


def window(integrals, eps_occ, eps_vir, src_occ, occ_offset, vir_offset):
    return pl.pallas_call(
        kernel,
        out_shape=jax.ShapeDtypeStruct((4, 512, 256), BF16),
        in_specs=[pl.BlockSpec(memory_space=pl.ANY)] * 3 + [pl.BlockSpec(memory_space=pltpu.SMEM)] * 3,
        out_specs=pl.BlockSpec(memory_space=pltpu.VMEM),
        scratch_shapes=[
            pltpu.VMEM((32, 64, 256), BF16),
            pltpu.VMEM((8, 128), F32),
            pltpu.VMEM((32, 128), F32),
            pltpu.VMEM((4, 4, 4, 2, 32, 128), BF16),
            pltpu.VMEM((4, 32, 256), BF16),
            pltpu.VMEM((128, 256), F32),
            pltpu.VMEM((4, 4, 4, 2, 32, 128), BF16),
            pltpu.VMEM((512, 1024), BF16),
            pltpu.VMEM((4, 4, 4, 2, 32, 256), BF16),
            pltpu.VMEM((4, 4, 4, 32, 256), BF16),
            pltpu.VMEM((16, 128, 256), F32),
            pltpu.VMEM((2, 8, Q, 128 // Q, 256), BF16),
            pltpu.VMEM((2, 8, Q, 128 // Q, 256), BF16),
            pltpu.VMEM((16, 2, 128, 256), BF16),
            pltpu.VMEM((4, 512, 256), F32),
            pltpu.SemaphoreType.DMA((COUNT,)),
            pltpu.SemaphoreType.DMA((COUNT,)),
        ],
        compiler_params=pltpu.CompilerParams(
            collective_id=0, has_side_effects=True, vmem_limit_bytes=55000000
        ),
        name="window",
    )(integrals, eps_occ.reshape(8, 128), eps_vir.reshape(32, 128), src_occ, occ_offset, vir_offset)


def local(*args):
    return window(*args).transpose(1, 0, 2)


def solution(mesh):
    in_specs = (P(("aux", "occ"), None, None), P(), P(), P(), P(), P())
    out_specs = P("aux", "occ", None)
    return jax.shard_map(local, mesh=mesh, in_specs=in_specs, out_specs=out_specs, check_vma=False)
```

```python
import jax
import jax.numpy as jnp
from jax import lax
from jax.experimental import pallas as pl
from jax.experimental.pallas import tpu as pltpu
from jax.sharding import PartitionSpec as P

MESH = pl.DeviceIdType.MESH
F32, BF16 = jnp.float32, jnp.bfloat16

Q = 4
SIZES = dict(A=96, SRC1=6, SRC2=6, FWD=8, ZG=4, XG=3, RING=16 * Q, AZ=3, AY=12, AR=8, AC=16, BY=3, BZ=12, BC=16, LOCAL=3)
SLOT, COUNT = {}, 0
for _name, _size in SIZES.items():
    SLOT[_name] = COUNT
    COUNT += _size
ORDER = (1, 3, 2)
CHUNKS = ((0, 1), (1, 3), (3, 4))


def coords():
    occ, aux = lax.axis_index("occ"), lax.axis_index("aux")
    return occ // 4, (aux // 2) % 4, (occ % 4) * 4 + aux // 8, aux % 2


def device(x, y, z, c):
    return {"occ": x * 4 + z // 4, "aux": ((z % 4) * 4 + y) * 2 + c}


def place(delta):
    low, high = delta % 2, delta // 2
    return 3 - 2 * low - 3 * high + 4 * low * high


def kernel(
    a_ref, eo_ref, ev_ref, so_ref, oo_ref, vo_ref, d_ref,
    arel, own_s, den, ar, at, sr, sd, cc, rb, sb, amp, dacc, snd, rcv,
):
    x, y, z, c = coords()
    zh, zl = z // 4, z % 4
    sends = []

    def copy(src, dst, slot, dev):
        return pltpu.make_async_remote_copy(
            src_ref=src, dst_ref=dst, send_sem=snd.at[slot], recv_sem=rcv.at[slot],
            device_id=dev, device_id_type=MESH,
        )

    def start(cp):
        cp.start()
        sends.append(cp)
        return cp

    barrier = pltpu.get_barrier_semaphore()

    def greet(dev):
        pl.semaphore_signal(barrier, inc=1, device_id=dev, device_id_type=MESH)

    greet(device(x, y, (z + 4) % 16, c))
    greet(device(x, y, (z + 12) % 16, c))

    @pl.loop(1, 32)
    def _(o):
        greet(device((x + o // 8) % 4, (y + (o // 2) % 4) % 4, z, (c + o) % 2))

    greet(device(x, y, (z + 1) % 16, c))
    greet(device(x, y, (z + 15) % 16, c))
    for j in ORDER:
        greet(device(x, y, zh * 4 + (zl + j) % 4, c))

    @pl.loop(0, 4)
    def _(tx):
        rows = a_ref[:, pl.ds(pl.multiple_of(tx * 16, 16), 16), :]
        turned = jnp.swapaxes(rows, 0, 1)
        for h in range(4):
            pos = place((h + 4 - zh) % 4)
            for ty in range(4):
                for tc in range(2):
                    arel[tx, pos, ty, tc] = turned[h * 4 + ty][:, tc * 128:(tc + 1) * 128]

    for s in range(4):
        j = so_ref[s]
        pos = place(((j // 4) % 4 + 4 - zh) % 4)
        for tc in range(2):
            own_s[s, :, tc * 128:(tc + 1) * 128] = arel[j // 16, pos, j % 4, tc]

    pl.semaphore_wait(barrier, 38)

    local = [
        pltpu.make_async_copy(arel.at[x, :, y, c], ar.at[:, x, y, c], rcv.at[SLOT["LOCAL"]]),
        pltpu.make_async_copy(own_s, sr.at[:, x, y, c], rcv.at[SLOT["LOCAL"] + 1]),
        pltpu.make_async_copy(own_s, sd.at[:, x, zh], rcv.at[SLOT["LOCAL"] + 2]),
    ]
    for cp in local:
        cp.start()

    xs = {j: (x + j) % 4 for j in (1, 2, 3)}
    ys = {j: (y + j) % 4 for j in (1, 2, 3)}
    src1 = []
    for j in ORDER:
        src1.append(start(copy(own_s.at[0:2], sr.at[0:2, x, y, c], SLOT["SRC1"] + j - 1, device(xs[j], y, z, c))))
        src1.append(start(copy(own_s.at[2:4], sr.at[2:4, x, y, c], SLOT["SRC1"] + 2 + j, device(x, ys[j], z, c))))
    up4, down4 = device(x, y, (z + 4) % 16, c), device(x, y, (z + 12) % 16, c)
    zg = [
        start(copy(own_s, sd.at[:, x, zh], SLOT["ZG"], up4)),
        start(copy(own_s, sd.at[:, x, zh], SLOT["ZG"] + 1, down4)),
    ]

    def a_copy(o, chunk):
        lo, hi = CHUNKS[chunk]
        tx, ty, tc = (x + o // 8) % 4, (y + (o // 2) % 4) % 4, (c + o) % 2
        return copy(
            arel.at[tx, lo:hi, ty, tc], ar.at[lo:hi, x, y, c], SLOT["A"] + chunk * 32 + o, device(tx, ty, z, tc)
        )

    def a_each(chunk, act):
        @pl.loop(1, 32)
        def _(o):
            act(a_copy(o, chunk))

    a_each(0, lambda cp: cp.start())
    for cp in local:
        cp.wait()
    other = device(x, y, z, 1 - c)
    for cp in src1:
        cp.wait_recv()
    vx, vy = sr.at[0:2, :, y, c], sr.at[2:4, x, :, c]
    src2 = []
    for j in ORDER:
        src2.append(start(copy(vx, vx, SLOT["SRC2"] + j - 1, device(x, ys[j], z, c))))
        src2.append(start(copy(vy, vy, SLOT["SRC2"] + 2 + j, device(xs[j], y, z, c))))
    fwd = [start(copy(v, v, SLOT["FWD"] + n, other)) for n, v in enumerate((vx, vy))]
    a_each(1, lambda cp: cp.start())
    a_each(2, lambda cp: cp.start())
    first_occ, first_vir = oo_ref[0], vo_ref[0]
    e_occ = eo_ref[first_occ + (x * 4 + zh) * 4 + y]
    e_src = eo_ref[first_occ + so_ref[zl]]
    row, lane = first_vir // 128, first_vir % 128
    window = jnp.concatenate(
        [ev_ref[pl.ds(row, 1), :], ev_ref[pl.ds(row + 1, 1), :], ev_ref[pl.ds(jnp.minimum(row + 2, 31), 1), :]], axis=1
    )

    def column(count, offset):
        at_lane = lax.broadcasted_iota(jnp.int32, (count, 384), 1)
        wanted = lax.broadcasted_iota(jnp.int32, (count, 384), 0) + offset
        return jnp.sum(jnp.where(at_lane == wanted, window, 0.0), axis=1, keepdims=True)

    whole = column(256, lane)
    diagonal = lax.broadcasted_iota(jnp.int32, (256, 256), 0) == lax.broadcasted_iota(jnp.int32, (256, 256), 1)
    vir_b = jnp.sum(jnp.where(diagonal, whole, 0.0), axis=0, keepdims=True)
    den[...] = column(128, lane + c * 128) + vir_b - e_occ - e_src

    for n, j in enumerate(ORDER):
        for k, view in enumerate((sr.at[0:2, :, (y + 4 - j) % 4, c], sr.at[2:4, (x + 4 - j) % 4, :, c])):
            src2[2 * n + k].wait_recv()
            fwd.append(start(copy(view, view, SLOT["FWD"] + 2 + 2 * n + k, other)))

    for k, cp in enumerate(list(zg)):
        cp.wait_recv()
        view = sd.at[0:2, x, (zh + 3) % 4] if k == 0 else sd.at[2:4, x, (zh + 1) % 4]
        zg.append(start(copy(view, view, SLOT["ZG"] + 2 + k, (up4, down4)[k])))

    def pairs(chunk, wait=()):
        lo, hi = CHUNKS[chunk]
        a_each(chunk, lambda cp: cp.wait_recv())
        for h in range(lo, hi):
            at[h * 128:(h + 1) * 128, :] = ar[h].reshape(1024, 128).T
        for cp in wait:
            cp.wait_recv()

        @pl.loop(0, 4)
        def _(s):
            part = jnp.dot(at[lo * 128:hi * 128, :], sr[s].reshape(1024, 256), preferred_element_type=F32)
            for h in range(lo, hi):
                cc[h * 4 + s] = part[(h - lo) * 128:(h - lo + 1) * 128]

    up, down = device(x, y, (z + 1) % 16, c), device(x, y, (z + 15) % 16, c)
    span = 128 // Q

    def hop(way, d, q):
        slot = SLOT["RING"] + (way * 8 + d - 1) * Q + q
        return copy(sb.at[way, d - 1, q], rb.at[way, d - 1, q], slot, up if way == 0 else down)

    def send(way, d, q, add):
        ahead = d if way == 0 else 16 - d
        target = (z + ahead) % 16
        spot = place((target // 4 + 4 - zh) % 4) * 4 + target % 4
        value = cc[spot, pl.ds(q * span, span), :]
        if add:
            hop(way, d + 1, q).wait_recv()
            value = value + rb[way, d, q].astype(F32)
        sb[way, d - 1, q] = value.astype(BF16)
        hop(way, d, q).start()

    def steps(lo, hi):
        @pl.loop(lo, hi)
        def _(k):
            for q in range(Q):
                send(0, 8 - k, q, True)
                send(1, 7 - k, q, True)

    def flush():
        for chunk in range(3):
            a_each(chunk, lambda cp: cp.wait_send())
        for cp in sends:
            cp.wait_send()

    def flush_ring():
        for q in range(Q):
            hop(0, 8, q).wait_send()

            @pl.loop(1, 8)
            def _(d, q=q):
                hop(0, d, q).wait_send()
                hop(1, d, q).wait_send()

    pairs(0, fwd)
    for q in range(Q):
        send(0, 8, q, False)
    pairs(1)
    for q in range(Q):
        send(1, 7, q, False)
    steps(1, 4)
    pairs(2)
    for cp in zg[2:]:
        cp.wait_recv()
    vd = sd.at[:, x]
    xg = [start(copy(vd, vd, SLOT["XG"] + j - 1, device(xs[j], y, z, c))) for j in ORDER]
    steps(4, 7)
    for q in range(Q):
        send(0, 1, q, True)

    own = amp.at[y * 4 + zl, c]
    mine = place(0) * 4 + zl
    for q in range(Q):
        rows = pl.ds(q * span, span)
        hop(1, 1, q).wait_recv()
        total = cc[mine, rows, :] + rb[1, 0, q].astype(F32)
        hop(0, 1, q).wait_recv()
        total = total + rb[0, 0, q].astype(F32)
        own[rows, :] = (total / den[rows, :]).astype(BF16)

    most, rest = pl.ds(0, 96), pl.ds(96, 32)

    def block(j, m):
        return (y + 4 - m) % 4 * 4 + (zl + 4 - j) % 4

    def group(j):
        return device(x, y, zh * 4 + (zl + j) % 4, c)

    def to_z(j):
        view = amp.at[block(0, 0), c, most]
        return copy(view, view, SLOT["AZ"] + j - 1, group(j))

    def to_y(j, m):
        view = amp.at[block(j, 0), c, most]
        return copy(view, view, SLOT["AY"] + j * 3 + m - 1, device(x, ys[m], z, c))

    def relay(j, half):
        view = amp.at[block(j, (1, 3)[half]), c, pl.ds(half * 48, 48)]
        return copy(view, view, SLOT["AR"] + j * 2 + half, device(x, ys[(1, 3)[half]], z, c))

    def to_core(j, m):
        view = amp.at[block(j, m), c, most]
        return copy(view, view, SLOT["AC"] + j * 4 + m, other)

    def rest_y(m):
        view = amp.at[block(0, 0), c, rest]
        return copy(view, view, SLOT["BY"] + m - 1, device(x, ys[m], z, c))

    def rest_z(j, m):
        view = amp.at[block(0, m), c, rest]
        return copy(view, view, SLOT["BZ"] + (j - 1) * 4 + m, group(j))

    def rest_core(j, m):
        view = amp.at[block(j, m), c, rest]
        return copy(view, view, SLOT["BC"] + j * 4 + m, other)

    touched = set()

    def product(j, m, last=False):
        to_core(j, m).wait_recv()
        rest_core(j, m).wait_recv()
        b = block(j, m)
        t, s = b // 4, b % 4
        lhs, rhs = sd[s].reshape(512, 256), amp[b].reshape(256, 256)
        straight = lax.dot_general(lhs, rhs, (((1,), (1,)), ((), ())), preferred_element_type=F32)
        crossed = jnp.dot(lhs, rhs, preferred_element_type=F32)
        value = 2.0 * straight - crossed
        if m in touched:
            value = dacc[t] + value
        touched.add(m)
        if last:
            d_ref[t] = value.astype(BF16)
        else:
            dacc[t] = value

    turn, near = (0, 1, 3, 2), (0, 1, 3)
    for m in ORDER:
        start(rest_y(m))
    for k in (2, 1, 3):
        start(to_z(k))
    start(to_y(0, 1))
    start(to_y(0, 3))
    for k in (2, 1, 3):
        start(rest_z(k, 0))
    start(to_core(0, 0))
    start(rest_core(0, 0))
    for m in ORDER:
        rest_y(m).wait_recv()
        for k in (2, 1, 3):
            start(rest_z(k, m))
        start(rest_core(0, m))
    for j in turn[1:]:
        to_z(j).wait_recv()
        start(to_y(j, 1))
        start(to_y(j, 3))
        start(to_core(j, 0))
    for cp in xg:
        cp.wait_recv()
    for j in turn:
        for half, m in enumerate((1, 3)):
            to_y(j, m).wait_recv()
            start(relay(j, half))
            start(to_core(j, m))
        if j == 3:
            for m in near:
                product(0, m)

    def take(j):
        for half in range(2):
            relay(j, half).wait_recv()
        start(to_core(j, 2))

    take(0)
    for j in turn[1:]:
        for m in turn:
            rest_z(j, m).wait_recv()
            start(rest_core(j, m))
    for j in (1, 3):
        take(j)
        for m in near:
            product(j, m)
    take(2)
    for m in near:
        product(2, m, True)
    for j in turn:
        product(j, 2, j == 2)
    flush()
    flush_ring()


def window(integrals, eps_occ, eps_vir, src_occ, occ_offset, vir_offset):
    vmem, smem = pl.BlockSpec(memory_space=pltpu.VMEM), pl.BlockSpec(memory_space=pltpu.SMEM)
    return pl.pallas_call(
        kernel,
        out_shape=jax.ShapeDtypeStruct((4, 512, 256), BF16),
        in_specs=[vmem, smem, vmem, smem, smem, smem],
        out_specs=vmem,
        scratch_shapes=[
            pltpu.VMEM((4, 4, 4, 2, 32, 128), BF16),
            pltpu.VMEM((4, 32, 256), BF16),
            pltpu.VMEM((128, 256), F32),
            pltpu.VMEM((4, 4, 4, 2, 32, 128), BF16),
            pltpu.VMEM((512, 1024), BF16),
            pltpu.VMEM((4, 4, 4, 2, 32, 256), BF16),
            pltpu.VMEM((4, 4, 4, 32, 256), BF16),
            pltpu.VMEM((16, 128, 256), F32),
            pltpu.VMEM((2, 8, Q, 128 // Q, 256), BF16),
            pltpu.VMEM((2, 8, Q, 128 // Q, 256), BF16),
            pltpu.VMEM((16, 2, 128, 256), BF16),
            pltpu.VMEM((4, 512, 256), F32),
            pltpu.SemaphoreType.DMA((COUNT,)),
            pltpu.SemaphoreType.DMA((COUNT,)),
        ],
        compiler_params=pltpu.CompilerParams(
            collective_id=0, has_side_effects=True, vmem_limit_bytes=48 << 20
        ),
        name="window",
    )(integrals, eps_occ, eps_vir.reshape(32, 128), src_occ, occ_offset, vir_offset)


def local(*args):
    return window(*args).transpose(1, 0, 2)


def solution(mesh):
    in_specs = (P(("aux", "occ"), None, None), P(), P(), P(), P(), P())
    out_specs = P("aux", "occ", None)
    return jax.shard_map(local, mesh=mesh, in_specs=in_specs, out_specs=out_specs, check_vma=False)
```

```python
import jax
import jax.numpy as jnp
from jax import lax
from jax.experimental import pallas as pl
from jax.experimental.pallas import tpu as pltpu
from jax.sharding import PartitionSpec as P

MESH = pl.DeviceIdType.MESH
F32, BF16 = jnp.float32, jnp.bfloat16

Q = 4
SIZES = dict(A=96, SRC1=6, SRC2=6, FWD=8, ZG=4, XG=3, RING=16 * Q, AZ=3, AY=12, AR=8, AC=16, BY=3, BZ=12, BC=16, LOCAL=3)
SLOT, COUNT = {}, 0
for _name, _size in SIZES.items():
    SLOT[_name] = COUNT
    COUNT += _size
ORDER = (1, 3, 2)
CHUNKS = ((0, 1), (1, 3), (3, 4))


def coords():
    occ, aux = lax.axis_index("occ"), lax.axis_index("aux")
    return occ // 4, (aux // 2) % 4, (occ % 4) * 4 + aux // 8, aux % 2


def device(x, y, z, c):
    return {"occ": x * 4 + z // 4, "aux": ((z % 4) * 4 + y) * 2 + c}


def place(delta):
    low, high = delta % 2, delta // 2
    return 3 - 2 * low - 3 * high + 4 * low * high


def kernel(
    a_ref, eo_ref, ev_ref, so_ref, oo_ref, vo_ref, d_ref,
    arel, own_s, den, ar, at, sr, sd, cc, rb, sb, amp, dacc, snd, rcv,
):
    x, y, z, c = coords()
    zh, zl = z // 4, z % 4
    sends = []

    def copy(src, dst, slot, dev):
        return pltpu.make_async_remote_copy(
            src_ref=src, dst_ref=dst, send_sem=snd.at[slot], recv_sem=rcv.at[slot],
            device_id=dev, device_id_type=MESH,
        )

    def start(cp):
        cp.start()
        sends.append(cp)
        return cp

    barrier = pltpu.get_barrier_semaphore()

    def greet(dev):
        pl.semaphore_signal(barrier, inc=1, device_id=dev, device_id_type=MESH)

    greet(device(x, y, (z + 4) % 16, c))
    greet(device(x, y, (z + 12) % 16, c))

    @pl.loop(1, 32)
    def _(o):
        greet(device((x + o // 8) % 4, (y + (o // 2) % 4) % 4, z, (c + o) % 2))

    greet(device(x, y, (z + 1) % 16, c))
    greet(device(x, y, (z + 15) % 16, c))
    for j in ORDER:
        greet(device(x, y, zh * 4 + (zl + j) % 4, c))

    @pl.loop(0, 4)
    def _(tx):
        rows = a_ref[:, pl.ds(pl.multiple_of(tx * 16, 16), 16), :]
        turned = jnp.swapaxes(rows, 0, 1)
        for h in range(4):
            pos = place((h + 4 - zh) % 4)
            for ty in range(4):
                for tc in range(2):
                    arel[tx, pos, ty, tc] = turned[h * 4 + ty][:, tc * 128:(tc + 1) * 128]

    for s in range(4):
        j = so_ref[s]
        pos = place(((j // 4) % 4 + 4 - zh) % 4)
        for tc in range(2):
            own_s[s, :, tc * 128:(tc + 1) * 128] = arel[j // 16, pos, j % 4, tc]

    first_occ, first_vir = oo_ref[0], vo_ref[0]
    e_occ = eo_ref[first_occ + (x * 4 + zh) * 4 + y]
    e_src = eo_ref[first_occ + so_ref[zl]]
    row, lane = first_vir // 128, first_vir % 128
    window = jnp.concatenate(
        [ev_ref[pl.ds(row, 1), :], ev_ref[pl.ds(row + 1, 1), :], ev_ref[pl.ds(jnp.minimum(row + 2, 31), 1), :]], axis=1
    )

    def column(count, offset):
        at_lane = lax.broadcasted_iota(jnp.int32, (count, 384), 1)
        wanted = lax.broadcasted_iota(jnp.int32, (count, 384), 0) + offset
        return jnp.sum(jnp.where(at_lane == wanted, window, 0.0), axis=1, keepdims=True)

    whole = column(256, lane)
    diagonal = lax.broadcasted_iota(jnp.int32, (256, 256), 0) == lax.broadcasted_iota(jnp.int32, (256, 256), 1)
    vir_b = jnp.sum(jnp.where(diagonal, whole, 0.0), axis=0, keepdims=True)
    den[...] = column(128, lane + c * 128) + vir_b - e_occ - e_src

    pl.semaphore_wait(barrier, 38)

    local = [
        pltpu.make_async_copy(arel.at[x, :, y, c], ar.at[:, x, y, c], rcv.at[SLOT["LOCAL"]]),
        pltpu.make_async_copy(own_s, sr.at[:, x, y, c], rcv.at[SLOT["LOCAL"] + 1]),
        pltpu.make_async_copy(own_s, sd.at[:, x, zh], rcv.at[SLOT["LOCAL"] + 2]),
    ]
    for cp in local:
        cp.start()

    xs = {j: (x + j) % 4 for j in (1, 2, 3)}
    ys = {j: (y + j) % 4 for j in (1, 2, 3)}
    src1 = []
    for j in ORDER:
        src1.append(start(copy(own_s.at[0:2], sr.at[0:2, x, y, c], SLOT["SRC1"] + j - 1, device(xs[j], y, z, c))))
        src1.append(start(copy(own_s.at[2:4], sr.at[2:4, x, y, c], SLOT["SRC1"] + 2 + j, device(x, ys[j], z, c))))
    up4, down4 = device(x, y, (z + 4) % 16, c), device(x, y, (z + 12) % 16, c)
    zg = [
        start(copy(own_s, sd.at[:, x, zh], SLOT["ZG"], up4)),
        start(copy(own_s, sd.at[:, x, zh], SLOT["ZG"] + 1, down4)),
    ]

    def a_copy(o, chunk):
        lo, hi = CHUNKS[chunk]
        tx, ty, tc = (x + o // 8) % 4, (y + (o // 2) % 4) % 4, (c + o) % 2
        return copy(
            arel.at[tx, lo:hi, ty, tc], ar.at[lo:hi, x, y, c], SLOT["A"] + chunk * 32 + o, device(tx, ty, z, tc)
        )

    def a_each(chunk, act):
        @pl.loop(1, 32)
        def _(o):
            act(a_copy(o, chunk))

    a_each(0, lambda cp: cp.start())
    for cp in local:
        cp.wait()
    other = device(x, y, z, 1 - c)
    for cp in src1:
        cp.wait_recv()
    vx, vy = sr.at[0:2, :, y, c], sr.at[2:4, x, :, c]
    src2 = []
    for j in ORDER:
        src2.append(start(copy(vx, vx, SLOT["SRC2"] + j - 1, device(x, ys[j], z, c))))
        src2.append(start(copy(vy, vy, SLOT["SRC2"] + 2 + j, device(xs[j], y, z, c))))
    fwd = [start(copy(v, v, SLOT["FWD"] + n, other)) for n, v in enumerate((vx, vy))]
    a_each(1, lambda cp: cp.start())
    a_each(2, lambda cp: cp.start())
    for n, j in enumerate(ORDER):
        for k, view in enumerate((sr.at[0:2, :, (y + 4 - j) % 4, c], sr.at[2:4, (x + 4 - j) % 4, :, c])):
            src2[2 * n + k].wait_recv()
            fwd.append(start(copy(view, view, SLOT["FWD"] + 2 + 2 * n + k, other)))

    for k, cp in enumerate(list(zg)):
        cp.wait_recv()
        view = sd.at[0:2, x, (zh + 3) % 4] if k == 0 else sd.at[2:4, x, (zh + 1) % 4]
        zg.append(start(copy(view, view, SLOT["ZG"] + 2 + k, (up4, down4)[k])))

    def pairs(chunk, wait=()):
        lo, hi = CHUNKS[chunk]
        a_each(chunk, lambda cp: cp.wait_recv())
        for h in range(lo, hi):
            at[h * 128:(h + 1) * 128, :] = ar[h].reshape(1024, 128).T
        for cp in wait:
            cp.wait_recv()

        @pl.loop(0, 4)
        def _(s):
            part = jnp.dot(at[lo * 128:hi * 128, :], sr[s].reshape(1024, 256), preferred_element_type=F32)
            for h in range(lo, hi):
                cc[h * 4 + s] = part[(h - lo) * 128:(h - lo + 1) * 128]

    up, down = device(x, y, (z + 1) % 16, c), device(x, y, (z + 15) % 16, c)
    span = 128 // Q

    def hop(way, d, q):
        slot = SLOT["RING"] + (way * 8 + d - 1) * Q + q
        return copy(sb.at[way, d - 1, q], rb.at[way, d - 1, q], slot, up if way == 0 else down)

    def send(way, d, q, add):
        ahead = d if way == 0 else 16 - d
        target = (z + ahead) % 16
        spot = place((target // 4 + 4 - zh) % 4) * 4 + target % 4
        value = cc[spot, pl.ds(q * span, span), :]
        if add:
            hop(way, d + 1, q).wait_recv()
            value = value + rb[way, d, q].astype(F32)
        sb[way, d - 1, q] = value.astype(BF16)
        hop(way, d, q).start()

    def steps(lo, hi):
        @pl.loop(lo, hi)
        def _(k):
            for q in range(Q):
                send(0, 8 - k, q, True)
                send(1, 7 - k, q, True)

    def flush():
        for chunk in range(3):
            a_each(chunk, lambda cp: cp.wait_send())
        for cp in sends:
            cp.wait_send()

    def flush_ring():
        for q in range(Q):
            hop(0, 8, q).wait_send()

            @pl.loop(1, 8)
            def _(d, q=q):
                hop(0, d, q).wait_send()
                hop(1, d, q).wait_send()

    pairs(0, fwd)
    for q in range(Q):
        send(0, 8, q, False)
    pairs(1)
    for q in range(Q):
        send(1, 7, q, False)
    steps(1, 4)
    pairs(2)
    for cp in zg[2:]:
        cp.wait_recv()
    vd = sd.at[:, x]
    xg = [start(copy(vd, vd, SLOT["XG"] + j - 1, device(xs[j], y, z, c))) for j in ORDER]
    steps(4, 7)
    for q in range(Q):
        send(0, 1, q, True)

    own = amp.at[y * 4 + zl, c]
    mine = place(0) * 4 + zl
    for q in range(Q):
        rows = pl.ds(q * span, span)
        hop(1, 1, q).wait_recv()
        total = cc[mine, rows, :] + rb[1, 0, q].astype(F32)
        hop(0, 1, q).wait_recv()
        total = total + rb[0, 0, q].astype(F32)
        own[rows, :] = (total / den[rows, :]).astype(BF16)

    most, rest = pl.ds(0, 96), pl.ds(96, 32)

    def block(j, m):
        return (y + 4 - m) % 4 * 4 + (zl + 4 - j) % 4

    def group(j):
        return device(x, y, zh * 4 + (zl + j) % 4, c)

    def to_z(j):
        view = amp.at[block(0, 0), c, most]
        return copy(view, view, SLOT["AZ"] + j - 1, group(j))

    def to_y(j, m):
        view = amp.at[block(j, 0), c, most]
        return copy(view, view, SLOT["AY"] + j * 3 + m - 1, device(x, ys[m], z, c))

    def relay(j, half):
        view = amp.at[block(j, (1, 3)[half]), c, pl.ds(half * 48, 48)]
        return copy(view, view, SLOT["AR"] + j * 2 + half, device(x, ys[(1, 3)[half]], z, c))

    def to_core(j, m):
        view = amp.at[block(j, m), c, most]
        return copy(view, view, SLOT["AC"] + j * 4 + m, other)

    def rest_y(m):
        view = amp.at[block(0, 0), c, rest]
        return copy(view, view, SLOT["BY"] + m - 1, device(x, ys[m], z, c))

    def rest_z(j, m):
        view = amp.at[block(0, m), c, rest]
        return copy(view, view, SLOT["BZ"] + (j - 1) * 4 + m, group(j))

    def rest_core(j, m):
        view = amp.at[block(j, m), c, rest]
        return copy(view, view, SLOT["BC"] + j * 4 + m, other)

    touched = set()

    def product(j, m, last=False):
        to_core(j, m).wait_recv()
        rest_core(j, m).wait_recv()
        b = block(j, m)
        t, s = b // 4, b % 4
        lhs, rhs = sd[s].reshape(512, 256), amp[b].reshape(256, 256)
        straight = lax.dot_general(lhs, rhs, (((1,), (1,)), ((), ())), preferred_element_type=F32)
        crossed = jnp.dot(lhs, rhs, preferred_element_type=F32)
        value = 2.0 * straight - crossed
        if m in touched:
            value = dacc[t] + value
        touched.add(m)
        if last:
            d_ref[t] = value.astype(BF16)
        else:
            dacc[t] = value

    turn, near = (0, 1, 3, 2), (0, 1, 3)
    for m in ORDER:
        start(rest_y(m))
    for k in (2, 1, 3):
        start(to_z(k))
    start(to_y(0, 1))
    start(to_y(0, 3))
    for k in (2, 1, 3):
        start(rest_z(k, 0))
    start(to_core(0, 0))
    start(rest_core(0, 0))
    for m in ORDER:
        rest_y(m).wait_recv()
        for k in (2, 1, 3):
            start(rest_z(k, m))
        start(rest_core(0, m))
    for j in turn[1:]:
        to_z(j).wait_recv()
        start(to_y(j, 1))
        start(to_y(j, 3))
        start(to_core(j, 0))
    for cp in xg:
        cp.wait_recv()
    for j in turn:
        for half, m in enumerate((1, 3)):
            to_y(j, m).wait_recv()
            start(relay(j, half))
            start(to_core(j, m))
        if j == 3:
            for m in near:
                product(0, m)

    def take(j):
        for half in range(2):
            relay(j, half).wait_recv()
        start(to_core(j, 2))

    take(0)
    for j in turn[1:]:
        for m in turn:
            rest_z(j, m).wait_recv()
            start(rest_core(j, m))
    for j in (1, 3):
        take(j)
        for m in near:
            product(j, m)
    take(2)
    for m in near:
        product(2, m, True)
    for j in turn:
        product(j, 2, j == 2)
    flush()
    flush_ring()


def window(integrals, eps_occ, eps_vir, src_occ, occ_offset, vir_offset):
    vmem, smem = pl.BlockSpec(memory_space=pltpu.VMEM), pl.BlockSpec(memory_space=pltpu.SMEM)
    return pl.pallas_call(
        kernel,
        out_shape=jax.ShapeDtypeStruct((4, 512, 256), BF16),
        in_specs=[vmem, smem, vmem, smem, smem, smem],
        out_specs=vmem,
        scratch_shapes=[
            pltpu.VMEM((4, 4, 4, 2, 32, 128), BF16),
            pltpu.VMEM((4, 32, 256), BF16),
            pltpu.VMEM((128, 256), F32),
            pltpu.VMEM((4, 4, 4, 2, 32, 128), BF16),
            pltpu.VMEM((512, 1024), BF16),
            pltpu.VMEM((4, 4, 4, 2, 32, 256), BF16),
            pltpu.VMEM((4, 4, 4, 32, 256), BF16),
            pltpu.VMEM((16, 128, 256), F32),
            pltpu.VMEM((2, 8, Q, 128 // Q, 256), BF16),
            pltpu.VMEM((2, 8, Q, 128 // Q, 256), BF16),
            pltpu.VMEM((16, 2, 128, 256), BF16),
            pltpu.VMEM((4, 512, 256), F32),
            pltpu.SemaphoreType.DMA((COUNT,)),
            pltpu.SemaphoreType.DMA((COUNT,)),
        ],
        compiler_params=pltpu.CompilerParams(
            collective_id=0, has_side_effects=True, vmem_limit_bytes=48 << 20
        ),
        name="window",
    )(integrals, eps_occ, eps_vir.reshape(32, 128), src_occ, occ_offset, vir_offset)


def local(*args):
    return window(*args).transpose(1, 0, 2)


def solution(mesh):
    in_specs = (P(("aux", "occ"), None, None), P(), P(), P(), P(), P())
    out_specs = P("aux", "occ", None)
    return jax.shard_map(local, mesh=mesh, in_specs=in_specs, out_specs=out_specs, check_vma=False)
```
